32 devices in a mesh: lat: 4 (over z), fld: 4 (over y, x), rep: 2 (over core).
Axes of the slice: x: 2, y: 2, z: 4, core: 2. Of those that a mesh axis runs over, the one named last changes fastest.
Arguments:
- field: float32 [12, 1280, 2560], P('fld', ('lat', 'rep')), may hold values from -6 to 6
- wind_zonal: float32 [12, 1280, 2560], P('fld', ('lat', 'rep')), may hold values from -4 to 4
- wind_merid: float32 [12, 1280, 2560], P('fld', ('lat', 'rep')), may hold values from -4 to 4
- band: int32 [12, 2], replicated, may hold values from 0 to 1280, as said below
- waves: int32 [16, 80], replicated, may hold values from -1 to 1279, as said below
- legendre: bfloat16 [16, 1280, 51328], P(('lat', 'fld')), may hold values from -0.15625 to 0.15625
Outputs:
- spectrum: float32 [16, 12, 2, 51328], P(('lat', 'fld'), 'rep')
The draws below stay inside these ranges and needn't reach their ends.
Inputs may be any that keep to these rules, and one draw needn't show every extreme that they name: band[f, 0] is below 320 and band[f, 1] is above 960, for every field-level. `waves`: every wavenumber 0 to 1279 stands in exactly one slot of one group; -1 marks an empty slot. Wavenumber m takes 1280 - m columns, and the wavenumbers of one group take at most 51240 columns together; some group takes exactly 51240.
All inputs are finite; a program needn't handle non-finite values.
Results may differ from the reference program's by a relative error of at most 0.0056.
Values may be sent and summed in bfloat16 or wider, within the bound.
A program may use at most 256 MiB of HBM per device.

```python
import math
import jax
import jax.numpy as jnp
from jax import lax

NLAT = 1280
NLON = 2560
M = 1280
F = 12
GROUPS = 16
ROUNDS = 40
REST = 0
SLOTS = 80
COLS = 51328


def draw_band(key, part):
    keys = jax.random.split(jax.random.fold_in(key, 11), 4)
    quarter = NLAT // 4
    lower_rows = jax.random.randint(keys[0], (F,), 0, quarter)
    upper_rows = NLAT - jax.random.randint(keys[1], (F,), 0, quarter)
    lower_rows = lower_rows.at[jax.random.randint(keys[2], (), 0, F)].set(0)
    upper_rows = upper_rows.at[jax.random.randint(keys[3], (), 0, F)].set(NLAT)
    return jnp.stack([lower_rows, upper_rows], axis=1).astype(jnp.int32)


def draw_waves(key, part):
    base_key = jax.random.fold_in(key, 23)
    assignment = -jnp.ones((GROUPS, SLOTS), jnp.int32)
    positions = jnp.arange(GROUPS, dtype=jnp.int32)
    for round_index in range(ROUNDS):
        ordering = jax.random.permutation(jax.random.fold_in(base_key, round_index), GROUPS)
        first_waves = 2 * round_index * GROUPS + positions
        second_waves = (2 * round_index + 2) * GROUPS - 1 - positions
        assignment = assignment.at[ordering, 2 * round_index].set(first_waves)
        assignment = assignment.at[ordering, 2 * round_index + 1].set(second_waves)
    if REST > 0:
        ordering = jax.random.permutation(jax.random.fold_in(base_key, ROUNDS + 7), GROUPS)
        rest_waves = jnp.where(positions < REST, 2 * ROUNDS * GROUPS + positions, -1).astype(jnp.int32)
        assignment = assignment.at[ordering, 2 * ROUNDS].set(rest_waves)
    slot_scores = jax.random.randint(jax.random.fold_in(base_key, 5003), (GROUPS, SLOTS), 0, 1 << 20)
    slot_scores = slot_scores * SLOTS + jnp.arange(SLOTS, dtype=jnp.int32)[None, :]
    shuffle = jnp.argsort(slot_scores, axis=1)
    return jnp.take_along_axis(assignment, shuffle, axis=1).astype(jnp.int32)


def block_levels(key, shape, cuts, low, largest):
    def one(position, blocks):
        heights = jax.random.uniform(jax.random.fold_in(jax.random.fold_in(key, 6), position), (blocks,), jnp.float32, low / len(cuts), largest / len(cuts))
        return jnp.repeat(jnp.exp(heights), shape[position] // blocks).reshape((-1,) + (1,) * (len(shape) - position - 1))

    loudness = one(*cuts[0])
    for cut in cuts[1:]:
        loudness = loudness * one(*cut)
    return loudness


def scatter_about(stream_key, dims, scale, limit, shards=(), held_as=jnp.bfloat16):
    drawn = jax.random.normal(stream_key, dims, jnp.float32) * scale
    if len(shards) > 0:
        drawn = block_levels(stream_key, dims, shards, -0.22, 0.18) * drawn
    return jnp.clip(drawn, min=-limit, max=limit).astype(held_as)


def setup_inputs(seed: int = 0) -> dict:
    seeds = jax.random.split(jax.random.key(seed), 7)
    field = scatter_about(seeds[0], (F, NLAT, NLON), 1.0, 6.0, ((0, 4), (1, 8)), jnp.float32)
    wind_zonal = scatter_about(seeds[1], (F, NLAT, NLON), 1.0, 4.0, ((0, 4), (1, 8)), jnp.float32)
    wind_merid = scatter_about(seeds[2], (F, NLAT, NLON), 1.0, 4.0, ((0, 4), (1, 8)), jnp.float32)
    band = draw_band(jax.random.fold_in(seeds[6], 71), 0)
    waves = draw_waves(jax.random.fold_in(seeds[6], 71), 0)
    legendre = scatter_about(seeds[5], (GROUPS, NLAT, COLS), NLAT ** -0.5, 0.15625, ((0, 16),))
    return {"field": field, "wind_zonal": wind_zonal, "wind_merid": wind_merid, "band": band, "waves": waves, "legendre": legendre}


def dft_matrix(lon_count, wave_count):
    lon_ids = lax.broadcasted_iota(jnp.int32, (lon_count, wave_count), 0)
    wave_ids = lax.broadcasted_iota(jnp.int32, (lon_count, wave_count), 1)
    angles = (lon_ids * wave_ids % lon_count).astype(jnp.float32) * (2.0 * math.pi / lon_count)
    scaling = 1.0 / math.sqrt(lon_count)
    return jnp.concatenate([jnp.cos(angles) * scaling, -jnp.sin(angles) * scaling], axis=1).astype(jnp.bfloat16)

def tendency(centre, above_row, below_row, zonal_wind, merid_wind):
    eastward = jnp.roll(centre, -1, axis=-1)
    westward = jnp.roll(centre, 1, axis=-1)
    return -(zonal_wind + centre) * (eastward - westward) * 0.5 - merid_wind * (above_row - below_row) * 0.5

def reference(field, wind_zonal, wind_merid, band, waves, legendre):
    matrix = dft_matrix(NLON, M)
    row_ids = jnp.arange(NLAT).astype(jnp.int32)[:, None]

    def one_field(inputs):
        values, zonal_wind, merid_wind, bounds = inputs
        in_band = ((row_ids >= bounds[0]) & (row_ids < bounds[1])).astype(jnp.float32)
        padded = jnp.pad(values, ((1, 1), (0, 0)))
        first_section = values + in_band * tendency(values, padded[2:], padded[:-2], zonal_wind, merid_wind)
        padded_section = jnp.pad(first_section, ((1, 1), (0, 0)))
        advected = 0.5 * (values + first_section + in_band * tendency(first_section, padded_section[2:], padded_section[:-2], zonal_wind, merid_wind))
        grid_low = advected.astype(jnp.bfloat16)
        return jnp.dot(grid_low, matrix, preferred_element_type=jnp.float32).astype(jnp.bfloat16)
    spectra = lax.map(one_field, (field, wind_zonal, wind_merid, band))
    spectra = spectra.reshape(F, NLAT, 2, M)
    col_ids = jnp.arange(COLS).astype(jnp.int32)

    def one_group(inputs):
        own_waves, columns = inputs
        own_filled = own_waves >= 0
        wave_index = jnp.where(own_filled, own_waves, 0).astype(jnp.int32)
        counts = jnp.where(own_filled, M - own_waves, 0).astype(jnp.int32)
        offsets = (jnp.cumsum(counts) - counts).astype(jnp.int32)
        segments = ((col_ids[None, :] >= offsets[:, None]) & (col_ids[None, :] < (offsets + counts)[:, None])).astype(jnp.float32)
        picked = jnp.take(spectra, wave_index, axis=3).astype(jnp.float32)
        products = jnp.einsum('flcs,lk->sfck', picked, columns.astype(jnp.float32))
        return jnp.einsum('sfck,sk->fck', products, segments)
    return lax.map(one_group, (waves, legendre))
```

```python
import functools
import math

import jax
import jax.numpy as jnp
from jax import lax
from jax.experimental import pallas as pl
from jax.experimental.pallas import tpu as pltpu
from jax.sharding import PartitionSpec as P

M = 1280
LANES = 128
PAD = 8
CHUNK = 16


def with_halo(value, sides, width):
    for axis, dim in sides:
        peers, length = (lax.axis_size(axis), value.shape[dim])
        up = [(i, (i + 1) % peers) for i in range(peers - 1)]
        down = [(j, i) for i, j in up]
        last = lax.slice_in_dim(value, length - width, length, axis=dim)
        first = lax.slice_in_dim(value, 0, width, axis=dim)
        before = lax.ppermute(last, axis, up)
        after = lax.ppermute(first, axis, down)
        value = jnp.concatenate([before, value, after], axis=dim)
    return value


def dft_matrix(lon_count, wave_count):
    lon_ids = lax.broadcasted_iota(jnp.int32, (lon_count, wave_count), 0)
    wave_ids = lax.broadcasted_iota(jnp.int32, (lon_count, wave_count), 1)
    angles = (lon_ids * wave_ids % lon_count).astype(jnp.float32) * (2.0 * math.pi / lon_count)
    scaling = 1.0 / math.sqrt(lon_count)
    return jnp.concatenate([jnp.cos(angles) * scaling, -jnp.sin(angles) * scaling], axis=1).astype(
        jnp.bfloat16
    )


def tendency(centre, above_row, below_row, zonal_wind, merid_wind):
    eastward = jnp.roll(centre, -1, axis=-1)
    westward = jnp.roll(centre, 1, axis=-1)
    return (
        -(zonal_wind + centre) * (eastward - westward) * 0.5
        - merid_wind * (above_row - below_row) * 0.5
    )


def band_mask(bounds, first_row, row_total):
    row_ids = first_row + lax.broadcasted_iota(jnp.int32, (1, row_total, 1), 1)
    lower_edge = bounds[:, 0][:, None, None]
    upper_edge = bounds[:, 1][:, None, None]
    return ((row_ids >= lower_edge) & (row_ids < upper_edge)).astype(jnp.float32)


SUB = 256
WIDE = 4096
HELD = 2


def angle_tables(waves, lon_count):
    groups, slots = waves.shape
    wave_column = jnp.where(waves >= 0, waves, 0).reshape(groups * slots, 1)
    lane = lax.broadcasted_iota(jnp.int32, (1, LANES), 1)
    quarter = lon_count // 4

    def cos_sin(step, scale):
        turns = (wave_column * ((step * lane) % lon_count)) % lon_count
        nearest = (2 * turns + quarter) // (2 * quarter)
        angle = (turns - nearest * quarter).astype(jnp.float32) * (2.0 * math.pi / lon_count)
        square = angle * angle
        cosine = 1.0 + square * (
            -0.5 + square * (1.0 / 24 + square * (-1.0 / 720 + square * (1.0 / 40320 - square / 3628800)))
        )
        sine = angle * (
            1.0 + square * (-1.0 / 6 + square * (1.0 / 120 + square * (-1.0 / 5040 + square / 362880)))
        )
        turn = nearest % 4
        odd = turn % 2 == 1
        cos_sign = jnp.where((turn == 1) | (turn == 2), -scale, scale)
        sin_sign = jnp.where(turn >= 2, -scale, scale)
        return jnp.where(odd, sine, cosine) * cos_sign, jnp.where(odd, cosine, sine) * sin_sign

    return cos_sin(1, 1.0) + cos_sin(LANES, 1.0 / math.sqrt(lon_count))


def spread_kernel(
    sizes, cuts, band, edges, low_cos, low_sin, high_cos, high_sin, field, zonal_in, merid_in, received,
    padded, zonal, merid, halo, halo_edges, section, grid_low, matrix, staged,
    load_sem, halo_send, halo_recv, send_sem, recv_sem,
):
    lat_size, fld_size, rep_size = sizes
    lat, fld, rep = lax.axis_index("lat"), lax.axis_index("fld"), lax.axis_index("rep")
    levels, rows, length = zonal.shape
    slots = matrix.shape[1] // 2
    groups = lat_size * fld_size
    half = lat_size // 2
    place = lat * fld_size + fld
    own_band = lat * rep_size + rep
    bands = lat_size * rep_size
    start = own_band * rows

    def load(level, which):
        ref, into = (
            (field, padded.at[level, pl.ds(PAD, rows)]),
            (zonal_in, zonal.at[level]),
            (merid_in, merid.at[level]),
        )[which]
        return pltpu.make_async_copy(ref.at[level], into, load_sem.at[level, which])

    for level in range(levels):
        for which in range(3):
            load(level, which).start()

    def halo_copy(side):
        other = own_band + (1 if side == 0 else -1)
        return pltpu.make_async_remote_copy(
            src_ref=edges.at[side],
            dst_ref=halo.at[side],
            send_sem=halo_send.at[side],
            recv_sem=halo_recv.at[side],
            device_id=(other // rep_size, fld, other % rep_size),
            device_id_type=pl.DeviceIdType.MESH,
        )

    is_first, is_last = own_band == 0, own_band == bands - 1

    @pl.when(jnp.logical_not(is_last))
    def _():
        halo_copy(0).start()

    @pl.when(jnp.logical_not(is_first))
    def _():
        halo_copy(1).start()

    @pl.when(is_first)
    def _():
        halo[0] = jnp.zeros(halo.shape[1:], halo.dtype)

    @pl.when(is_last)
    def _():
        halo[1] = jnp.zeros(halo.shape[1:], halo.dtype)

    @pl.when(jnp.logical_not(is_first))
    def _():
        halo_copy(0).wait_recv()

    @pl.when(jnp.logical_not(is_last))
    def _():
        halo_copy(1).wait_recv()

    def turned(value):
        return pltpu.roll(value, length - 1, axis=1), pltpu.roll(value, 1, axis=1)

    def neighbours(ref, first_row):
        value = ref[pl.ds(first_row, 2 * PAD + CHUNK), :]
        return tuple(value[PAD + shift : PAD + shift + CHUNK] for shift in (-1, 0, 1))

    def advect(level):
        for which in range(3):
            load(level, which).wait()
        lower = band[fld * levels + level, 0]
        upper = band[fld * levels + level, 1]

        def masked_slope(
            first_row, centre, turned_east, turned_west, next_row, previous, zonal_wind, merid_wind
        ):
            row_ids = start + first_row + lax.broadcasted_iota(jnp.int32, centre.shape, 0)
            in_band = ((row_ids >= lower) & (row_ids < upper)).astype(jnp.float32)
            return in_band * (
                -(zonal_wind + centre) * (turned_east - turned_west) * 0.5
                - merid_wind * (next_row - previous) * 0.5
            )

        here_padded = padded.at[level]
        here_padded[PAD - 2 : PAD, :] = halo[0, level, 0:2, :]
        here_padded[PAD + rows : PAD + rows + 2, :] = halo[1, level, 0:2, :]
        halo_edges[0:4, :] = halo[0, level]
        halo_edges[4:8, :] = halo[1, level]
        around = halo_edges[...]
        east, west = turned(around)
        section[PAD - 1 : PAD, :] = around[1:2] + masked_slope(
            -1, around[1:2], east[1:2], west[1:2], here_padded[PAD : PAD + 1, :], around[0:1],
            around[2:3], around[3:4],
        )
        section[PAD + rows : PAD + rows + 1, :] = around[4:5] + masked_slope(
            rows, around[4:5], east[4:5], west[4:5], around[5:6],
            here_padded[PAD + rows - 1 : PAD + rows, :], around[6:7], around[7:8],
        )

        @pl.loop(0, rows // CHUNK)
        def _(chunk):
            first_row = pl.multiple_of(chunk * CHUNK, CHUNK)
            here = pl.ds(first_row, CHUNK)
            previous, centre, next_row = neighbours(here_padded, first_row)
            section[pl.ds(pl.multiple_of(first_row + PAD, PAD), CHUNK), :] = centre + masked_slope(
                first_row, centre, *turned(centre), next_row, previous,
                zonal[level, here, :], merid[level, here, :],
            )

        @pl.loop(0, rows // CHUNK)
        def _(chunk):
            first_row = pl.multiple_of(chunk * CHUNK, CHUNK)
            here = pl.ds(first_row, CHUNK)
            previous, centre, next_row = neighbours(section, first_row)
            grid_low[pl.ds(pl.multiple_of(level * rows + first_row, CHUNK), CHUNK), :] = (
                0.5
                * (
                    here_padded[pl.ds(pl.multiple_of(first_row + PAD, PAD), CHUNK), :]
                    + centre
                    + masked_slope(
                        first_row, centre, *turned(centre), next_row, previous,
                        zonal[level, here, :], merid[level, here, :],
                    )
                )
            ).astype(jnp.bfloat16)

    def target_of(hop):
        turn = hop // fld_size
        crossing = turn < half
        side = jnp.where(crossing, 1 - lat // half, lat // half)
        within = jnp.where(crossing, lat + turn, lat + 1 + turn) % half
        return side * half + within, (fld + 1 + hop % fld_size) % fld_size

    def sending(hop, cut):
        to_lat, to_fld = target_of(hop)
        lanes = pl.ds(cuts[cut], cuts[cut + 1] - cuts[cut])
        return pltpu.make_async_remote_copy(
            src_ref=staged.at[hop, :, lanes],
            dst_ref=received.at[place, :, lanes],
            send_sem=send_sem.at[hop, cut],
            recv_sem=recv_sem.at[place, cut],
            device_id=(to_lat, to_fld, rep),
            device_id_type=pl.DeviceIdType.MESH,
        )

    def build(hop):
        to_lat, to_fld = target_of(hop)
        own_rows = pl.ds(pl.multiple_of((to_lat * fld_size + to_fld) * slots, 8), slots)
        near_cos, near_sin = low_cos[own_rows, :], low_sin[own_rows, :]
        far_cos, far_sin = high_cos[own_rows, :], high_sin[own_rows, :]
        for part in range(length // LANES):
            columns = slice(part * LANES, (part + 1) * LANES)
            scaled_cos = far_cos[:, part : part + 1]
            scaled_sin = far_sin[:, part : part + 1]
            matrix[hop, 0:slots, columns] = (
                scaled_cos * near_cos - scaled_sin * near_sin
            ).astype(jnp.bfloat16)
            matrix[hop, slots : 2 * slots, columns] = (
                -(scaled_sin * near_cos + scaled_cos * near_sin)
            ).astype(jnp.bfloat16)

    done = 0
    for cut in range(len(cuts) - 1):
        lanes = slice(cuts[cut], cuts[cut + 1])
        while done * rows < cuts[cut + 1]:
            advect(done)
            done += 1

        def step(hop, carry, cut=cut, lanes=lanes):
            if cut == 0:
                build(hop)
            staged[hop, :, lanes] = lax.dot_general(
                matrix[hop], grid_low[lanes, :], (((1,), (1,)), ((), ())),
                preferred_element_type=jnp.float32,
            ).astype(jnp.bfloat16)

            @pl.when(hop > 0)
            def _():
                sending(hop - 1, cut).start()

            return carry

        lax.fori_loop(0, groups, step, 0)
        received[place, :, lanes] = staged[groups - 1, :, lanes]

    @pl.when(jnp.logical_not(is_last))
    def _():
        halo_copy(0).wait_send()

    @pl.when(jnp.logical_not(is_first))
    def _():
        halo_copy(1).wait_send()

    for cut in range(len(cuts) - 1):

        def sent(hop, carry, cut=cut):
            sending(hop, cut).wait_send()
            return carry

        lax.fori_loop(0, groups - 1, sent, 0)
    for cut in range(len(cuts) - 1):
        lanes = pl.ds(cuts[cut], cuts[cut + 1] - cuts[cut])

        def arrived(step, carry, cut=cut, lanes=lanes):
            origin = (place + step) % groups
            pltpu.make_async_remote_copy(
                src_ref=staged.at[0, :, lanes],
                dst_ref=received.at[origin, :, lanes],
                send_sem=send_sem.at[0, cut],
                recv_sem=recv_sem.at[origin, cut],
                device_id=(lat, fld, 1 - rep),
                device_id_type=pl.DeviceIdType.MESH,
            ).wait_recv()
            return carry

        lax.fori_loop(1, groups, arrived, 0)


def spread(field, wind_zonal, wind_merid, band, waves, sizes):
    levels, rows, length = field.shape
    groups, slots = waves.shape
    winds = (wind_zonal, wind_merid)
    edges = jnp.stack(
        [
            jnp.concatenate([field[:, -2:]] + [w[:, -1:] for w in winds], axis=1),
            jnp.concatenate([field[:, :2]] + [w[:, :1] for w in winds], axis=1),
        ]
    )
    tables = angle_tables(waves, length)
    width = levels * rows
    full = width // LANES * LANES
    cuts = (0, LANES, 2 * LANES, width) if full >= 3 * LANES else (0, width)
    in_vmem = pl.BlockSpec(memory_space=pltpu.VMEM)
    in_hbm = pl.BlockSpec(memory_space=pl.ANY)
    return pl.pallas_call(
        functools.partial(spread_kernel, sizes, cuts),
        out_shape=jax.ShapeDtypeStruct((groups, 2 * slots, width), jnp.bfloat16),
        in_specs=[pl.BlockSpec(memory_space=pltpu.SMEM)] + [in_vmem] * 5 + [in_hbm] * 3,
        out_specs=in_vmem,
        scratch_shapes=[
            pltpu.VMEM((levels, rows + 2 * PAD, length), jnp.float32),
            pltpu.VMEM((levels, rows, length), jnp.float32),
            pltpu.VMEM((levels, rows, length), jnp.float32),
            pltpu.VMEM((2, levels, 4, length), jnp.float32),
            pltpu.VMEM((8, length), jnp.float32),
            pltpu.VMEM((rows + 2 * PAD, length), jnp.float32),
            pltpu.VMEM((width, length), jnp.bfloat16),
            pltpu.VMEM((groups, 2 * slots, length), jnp.bfloat16),
            pltpu.VMEM((groups, 2 * slots, width), jnp.bfloat16),
            pltpu.SemaphoreType.DMA((levels, 3)),
            pltpu.SemaphoreType.DMA((2,)),
            pltpu.SemaphoreType.DMA((2,)),
            pltpu.SemaphoreType.DMA((groups, len(cuts) - 1)),
            pltpu.SemaphoreType.DMA((groups, len(cuts) - 1)),
        ],
        compiler_params=pltpu.CompilerParams(has_side_effects=True, vmem_limit_bytes=52 << 20),
    )(band, edges, *tables, field, wind_zonal, wind_merid)


def legendre_kernel(
    lat_size, fld_size, field_count, first, last, starts, stops, own_rep, received, legendre,
    mine, theirs, ordered,
):
    tile = pl.program_id(0)
    width = mine.shape[1]
    slots = received.shape[1] // 2
    row_count = received.shape[2] // field_count
    depth = lat_size * row_count
    rows = fld_size * field_count * 2
    kept = rows // 2
    subs = width // SUB

    @pl.when(tile == 0)
    def _():
        for part in range(fld_size):
            fld = (part + own_rep[0] * (fld_size // 2)) % fld_size
            for level in range(field_count):
                for side in range(2):
                    row = (part * field_count + level) * 2 + side
                    piece = jnp.concatenate(
                        [
                            received[
                                lat * fld_size + fld,
                                side * slots : (side + 1) * slots,
                                level * row_count : (level + 1) * row_count,
                            ].astype(jnp.float32)
                            for lat in range(lat_size)
                        ],
                        axis=1,
                    )
                    for lane in range(depth // LANES):
                        ordered[lane, pl.ds(row, slots, stride=rows), :] = piece[
                            :, lane * LANES : (lane + 1) * LANES
                        ]

    def held(slot, columns):
        return (columns >= starts[slot]) & (columns < stops[slot])

    def taken(slot):
        at = jnp.minimum(slot, slots - 1) * rows
        here = pl.ds(pl.multiple_of(at, 8), rows)
        return jnp.concatenate(
            [ordered[lane, here, :] for lane in range(depth // LANES)], axis=1
        ).astype(jnp.bfloat16)

    for sub in range(subs):
        begin = first[tile * subs + sub]
        own = slice(sub * SUB, (sub + 1) * SUB)
        columns = tile * width + sub * SUB + lax.broadcasted_iota(jnp.int32, (1, SUB), 1)
        products = jnp.dot(
            jnp.concatenate([taken(begin + i) for i in range(HELD)], axis=0),
            legendre[0, :, 0, :, own].reshape(depth, SUB),
            preferred_element_type=jnp.float32,
        )
        total = jnp.where(held(begin, columns), products[0:rows], 0.0)
        for i in range(1, HELD):
            total = total + jnp.where(held(begin + i, columns), products[i * rows : (i + 1) * rows], 0.0)
        mine[:, own] = total[0:kept]
        theirs[:, own] = total[kept:rows].astype(theirs.dtype)

    @pl.loop(0, subs)
    def _(sub):
        begin = first[tile * subs + sub]
        end = last[tile * subs + sub]

        @pl.loop(begin + HELD, end)
        def _(slot):
            own = pl.ds(pl.multiple_of(sub * SUB, SUB), SUB)
            columns = tile * width + sub * SUB + lax.broadcasted_iota(jnp.int32, (1, SUB), 1)
            products = jnp.dot(
                taken(slot),
                legendre[0, :, 0, :, own].reshape(depth, SUB),
                preferred_element_type=jnp.float32,
            )
            inside = held(slot, columns)
            mine[:, own] = jnp.where(inside, products[0:kept], mine[:, own])
            theirs[:, own] = jnp.where(
                inside, products[kept:rows], theirs[:, own].astype(jnp.float32)
            ).astype(theirs.dtype)


def legendre_halves(received, own_waves, legendre, field_count, lat_size, fld_size, rep_size, wave_total):
    slots = own_waves.shape[0]
    counts = jnp.where(own_waves >= 0, wave_total - own_waves, 0)
    lower = lax.broadcasted_iota(jnp.int32, (slots, slots), 1) <= lax.broadcasted_iota(
        jnp.int32, (slots, slots), 0
    )
    stops = jnp.sum(jnp.where(lower, counts[None, :], 0), axis=1)
    starts = stops - counts
    depth, col_count = legendre.shape[1:]
    row_count = depth // (lat_size * rep_size)
    width = min(WIDE, pl.cdiv(col_count, SUB) * SUB)
    tiles = pl.cdiv(col_count, width)
    edges = jnp.arange(tiles * (width // SUB), dtype=jnp.int32)[:, None] * SUB
    first = jnp.sum((stops[None, :] <= edges).astype(jnp.int32), axis=1)
    last = jnp.sum((starts[None, :] < edges + SUB).astype(jnp.int32), axis=1)
    spare = ((0, HELD),)
    rows = fld_size * field_count * 2
    view = legendre.reshape(1, lat_size, rep_size, row_count, col_count)
    return pl.pallas_call(
        functools.partial(legendre_kernel, lat_size, fld_size, field_count),
        out_shape=(
            jax.ShapeDtypeStruct((rows // 2, col_count), jnp.float32),
            jax.ShapeDtypeStruct((rows // 2, col_count), jnp.bfloat16),
        ),
        grid_spec=pltpu.PrefetchScalarGridSpec(
            num_scalar_prefetch=5,
            grid=(tiles,),
            in_specs=[
                pl.BlockSpec(memory_space=pltpu.VMEM),
                pl.BlockSpec(
                    (1, lat_size, 1, row_count, width), lambda t, a, b, c, d, rep: (0, 0, rep[0], 0, t)
                ),
            ],
            out_specs=[
                pl.BlockSpec((rows // 2, width), lambda t, *_: (0, t)),
                pl.BlockSpec((rows // 2, width), lambda t, *_: (0, t)),
            ],
            scratch_shapes=[pltpu.VMEM((depth // rep_size // LANES, slots * rows, LANES), jnp.float32)],
        ),
        compiler_params=pltpu.CompilerParams(vmem_limit_bytes=40 << 20),
    )(
        first, last, jnp.pad(starts, spare), jnp.pad(stops, spare),
        lax.axis_index("rep").reshape(1), received, view,
    )


def pair_kernel(mine, theirs, out, arrived, send_sem, recv_sem):
    lat, fld, rep = lax.axis_index("lat"), lax.axis_index("fld"), lax.axis_index("rep")
    copy = pltpu.make_async_remote_copy(
        src_ref=theirs,
        dst_ref=arrived,
        send_sem=send_sem,
        recv_sem=recv_sem,
        device_id=(lat, fld, 1 - rep),
        device_id_type=pl.DeviceIdType.MESH,
    )
    copy.start()
    copy.wait()
    for level in range(out.shape[1]):
        pair = slice(2 * level, 2 * level + 2)
        out[0, level] = mine[pair, :] + arrived[pair, :].astype(jnp.float32)


def pair_sums(mine, theirs):
    rows, col_count = mine.shape
    in_vmem = pl.BlockSpec(memory_space=pltpu.VMEM)
    return pl.pallas_call(
        pair_kernel,
        out_shape=jax.ShapeDtypeStruct((1, rows // 2, 2, col_count), jnp.float32),
        in_specs=[in_vmem] * 2,
        out_specs=in_vmem,
        scratch_shapes=[
            pltpu.VMEM(theirs.shape, theirs.dtype),
            pltpu.SemaphoreType.DMA,
            pltpu.SemaphoreType.DMA,
        ],
        compiler_params=pltpu.CompilerParams(has_side_effects=True, vmem_limit_bytes=32 << 20),
    )(mine, theirs)


def body(field, wind_zonal, wind_merid, band, waves, legendre):
    field_count, row_count, lon_count = field.shape
    lat_size = lax.axis_size("lat")
    fld_size = lax.axis_size("fld")
    rep_size = lax.axis_size("rep")
    first_row = (lax.axis_index("lat") * rep_size + lax.axis_index("rep")) * row_count
    slot_count = waves.shape[1]
    direct = (
        row_count % 16 == 0
        and slot_count % 16 == 0
        and lon_count % LANES == 0
        and lon_count // LANES <= LANES
        and lon_count % 4 == 0
        and rep_size == 2
        and lat_size % 2 == 0
        and fld_size % 2 == 0
        and fld_size * field_count * 2 % 8 == 0
        and lat_size * row_count % LANES == 0
        and lat_size * fld_size <= 64
    )
    if direct:
        received = spread(
            field, wind_zonal, wind_merid, band, waves, (lat_size, fld_size, rep_size)
        )
        group = lax.axis_index("lat") * fld_size + lax.axis_index("fld")
        own_waves = lax.dynamic_index_in_dim(waves, group, 0, keepdims=False)
        mine, theirs = legendre_halves(
            received, own_waves, legendre, field_count, lat_size, fld_size, rep_size, M
        )
        return pair_sums(mine, theirs)
    bounds = lax.dynamic_slice_in_dim(band, lax.axis_index("fld") * field_count, field_count, 0)
    in_band = band_mask(bounds, first_row, row_count)
    padded = with_halo(field, ((("lat", "rep"), 1),), 1)
    first_section = field + in_band * tendency(
        field, padded[:, 2:], padded[:, :-2], wind_zonal, wind_merid
    )
    padded_section = with_halo(first_section, ((("lat", "rep"), 1),), 1)
    advected = 0.5 * (
        field
        + first_section
        + in_band
        * tendency(
            first_section, padded_section[:, 2:], padded_section[:, :-2], wind_zonal, wind_merid
        )
    )
    grid_low = advected.astype(jnp.bfloat16)
    spectra = jnp.dot(
        grid_low.reshape(field_count * row_count, lon_count),
        dft_matrix(lon_count, M),
        preferred_element_type=jnp.float32,
    ).astype(jnp.bfloat16)
    spectra = spectra.reshape(field_count, row_count, 2, M)
    wave_index = jnp.where(waves >= 0, waves, 0)
    picked = jnp.take(spectra, wave_index.reshape(-1), axis=3)
    picked = picked.reshape(field_count, row_count, 2, lat_size, fld_size, slot_count)
    outgoing = jnp.transpose(picked, (5, 2, 4, 0, 3, 1)).reshape(
        slot_count, 2, fld_size * field_count, lat_size * row_count
    )
    received = lax.all_to_all(
        lax.all_to_all(outgoing, "lat", split_axis=3, concat_axis=3, tiled=True),
        "fld",
        split_axis=2,
        concat_axis=2,
        tiled=True,
    )
    group = lax.axis_index("lat") * fld_size + lax.axis_index("fld")
    own_waves = lax.dynamic_index_in_dim(waves, group, 0, keepdims=False)
    counts = jnp.where(own_waves >= 0, M - own_waves, 0)
    offsets = jnp.cumsum(counts) - counts
    col_count = legendre.shape[2]
    col_ids = lax.broadcasted_iota(jnp.int32, (slot_count, col_count), 1)
    segments = ((col_ids >= offsets[:, None]) & (col_ids < (offsets + counts)[:, None])).astype(
        jnp.float32
    )
    total_fields = fld_size * field_count
    regrouped = lax.all_to_all(received, "rep", split_axis=2, concat_axis=3, tiled=True)
    half_fields = total_fields // rep_size
    ordered = regrouped.reshape(slot_count, 2, half_fields, rep_size, lat_size, row_count)
    ordered = jnp.transpose(ordered, (0, 1, 2, 4, 3, 5)).reshape(
        slot_count * 2 * half_fields, rep_size * lat_size * row_count
    )
    products = jnp.dot(ordered, legendre[0], preferred_element_type=jnp.float32)
    spectrum = jnp.einsum(
        "scfk,sk->fck", products.reshape(slot_count, 2, half_fields, col_count), segments
    )
    return spectrum[None]


def solution(mesh):
    placed = (
        P("fld", ("lat", "rep"), None),
        P("fld", ("lat", "rep"), None),
        P("fld", ("lat", "rep"), None),
        P(),
        P(),
        P(("lat", "fld"), None, None),
    )
    return jax.shard_map(
        body,
        mesh=mesh,
        in_specs=placed,
        out_specs=P(("lat", "fld"), "rep", None, None),
        check_vma=False,
    )
```
